32 devices in a mesh: band: 2 (over y), col: 8 (over z, x), disp: 2 (over core).
Axes of the slice: x: 2, y: 2, z: 4, core: 2. Of those that a mesh axis runs over, the one named last changes fastest.
Arguments:
- left_feat: bfloat16 [8, 32, 2048], P('band', None, 'col'), parts along dimension 0, may hold values from -6 to 6
- right_feat: bfloat16 [8, 32, 2048], P('band', None, 'col'), parts along dimension 0, may hold values from -6 to 6
- w_first: bfloat16 [3, 3, 3, 32, 64], replicated, may hold values from -0.15625 to 0.15625
- w_second: bfloat16 [3, 3, 3, 1, 32], replicated, may hold values from -0.625 to 0.625
Outputs:
- disparity: float32 [8, 2048], P('band', 'col'), parts along dimension 0
- confidence: float32 [8, 2048], P('band', 'col'), parts along dimension 0
The draws below stay inside these ranges and needn't reach their ends.
There are 2 independent parts, one for each index of `band`. The reference program is written for one: setup_inputs(seed, part) draws one part's arguments, and reference() takes and returns one part's arrays. A program takes and returns all parts, laid end to end along the dimension named above; an argument that names none is the same for every part. Nothing has to cross between parts.
All inputs are finite; a program needn't handle non-finite values.
Results may differ from the reference program's by a relative error of at most 0.0017.
Values may be sent and summed in bfloat16 or wider, within the bound.
A program may use at most 128 MiB of HBM per device.

```python
import jax
import jax.numpy as jnp
from jax import lax

FEAT = 32
CH = 64
HID = 32
DISP = 48
ROWS = 4
COL_DEV = 256
COLS = 2048


def level_of(own_key, extent, cuts, least, high):
    loudness = 1.0
    for dim, blocks in cuts:
        draws = jax.random.uniform(jax.random.fold_in(jax.random.fold_in(own_key, 6), dim), (blocks,), jnp.float32, least / len(cuts), high / len(cuts))
        loudness = loudness * jnp.repeat(jnp.exp(draws), extent[dim] // blocks).reshape((-1,) + (1,) * (len(extent) - 1 - dim))
    return loudness


def bell_draw(own_key, dims, scale, reach, split=(), kind=jnp.bfloat16):
    result = scale * jax.random.normal(own_key, dims, jnp.float32)
    if split:
        result = result * level_of(own_key, dims, split, -0.22, 0.18)
    return jnp.clip(result, -reach, reach).astype(kind)


def setup_inputs(seed: int = 0, part: int = 0) -> dict:
    key_list = jax.random.split(jax.random.key(seed), 5)
    part_splits = jax.random.split(jax.random.fold_in(key_list[4], part), 5)
    return {
        "left_feat": bell_draw(part_splits[0], (ROWS, FEAT, COLS), 1.0, 6.0, ((2, 8),)),
        "right_feat": bell_draw(part_splits[1], (ROWS, FEAT, COLS), 1.0, 6.0, ((2, 8),)),
        "w_first": bell_draw(key_list[2], (3, 3, 3, HID, CH), (27 * CH) ** -0.5, 0.15625),
        "w_second": bell_draw(key_list[3], (3, 3, 3, 1, HID), (3 * HID) ** -0.5, 0.625),
    }


def conv_three(field, kernel):
    out = lax.conv_general_dilated(field[None], kernel, (1, 1, 1), "VALID", dimension_numbers=("NDHCW", "DHWOI", "NDHCW"), preferred_element_type=jnp.float32)
    return out[0]


def reference(left_feat, right_feat, w_first, w_second):
    width = COL_DEV
    blocks = COLS // width
    left_pad = jnp.pad(left_feat, ((0, 0), (0, 0), (2, 2)))
    right_pad = jnp.pad(right_feat, ((0, 0), (0, 0), (DISP + 2, 2)))
    disp_ids = jnp.arange(DISP, dtype=jnp.int32)
    disp_vals = disp_ids.astype(jnp.float32)

    def one_block(index):
        start = (index * width).astype(jnp.int32)
        left_blk = lax.dynamic_slice_in_dim(left_pad, start, width + 4, 2)

        def right_for(shift_d):
            return lax.dynamic_slice_in_dim(right_pad, (start + DISP - shift_d).astype(jnp.int32), width + 4, 2)

        right_blk = jax.vmap(right_for)(disp_ids)
        columns = start - 2 + jnp.arange(width + 4, dtype=jnp.int32)
        inside = columns < COLS
        right_blk = jnp.where(inside[None, None, None, :], right_blk, jnp.zeros_like(right_blk))
        left_all = jnp.broadcast_to(left_blk[None], (DISP,) + left_blk.shape)
        volume = jnp.concatenate([left_all, right_blk], axis=2)
        volume = jnp.pad(volume, ((1, 1), (1, 1), (0, 0), (0, 0)))
        hidden = conv_three(volume, w_first)
        hid_cols = start - 1 + jnp.arange(width + 2, dtype=jnp.int32)
        keep = (hid_cols >= 0) & (hid_cols < COLS)
        hidden = jnp.where(keep[None, None, None, :], jax.nn.relu(hidden), jnp.float32(0.0)).astype(jnp.bfloat16)
        hidden = jnp.pad(hidden, ((1, 1), (1, 1), (0, 0), (0, 0)))
        cost = conv_three(hidden, w_second)[:, :, 0, :]
        expo = jnp.exp(-cost)
        total = jnp.sum(expo, axis=0)
        moment = jnp.sum(disp_vals[:, None, None] * expo, axis=0)
        soft = moment / total
        weights = jnp.maximum(jnp.float32(0.0), 1.0 - jnp.abs(soft[None] - disp_vals[:, None, None]))
        right_mid = right_blk[:, :, :, 2:width + 2].astype(jnp.float32)
        warped = jnp.einsum("drx,drcx->rcx", weights, right_mid)
        error = jnp.mean(jnp.abs(left_blk[:, :, 2:width + 2].astype(jnp.float32) - warped), axis=1)
        return soft / DISP, jnp.exp(-error)

    disp_b, conf_b = lax.map(one_block, jnp.arange(blocks, dtype=jnp.int32))
    disparity = jnp.transpose(disp_b, (1, 0, 2)).reshape(ROWS, COLS)
    confidence = jnp.transpose(conf_b, (1, 0, 2)).reshape(ROWS, COLS)
    return (disparity, confidence)
```

```python
import functools

import jax
import jax.numpy as jnp
from jax import lax
from jax.experimental import pallas as pl
from jax.experimental.pallas import tpu as pltpu
from jax.sharding import PartitionSpec as P

DISP = 48
NEG = -1e30
NT = (((1,), (1,)), ((), ()))
MESH = pl.DeviceIdType.MESH


def banded(block, lane):
    return [
        jnp.where(lane < 64, pltpu.roll(block, 96, 1), 0.0),
        block,
        pltpu.roll(block, 32, 1),
        jnp.where(lane >= 64, pltpu.roll(block, 64, 1), 0.0),
    ]


def kernel(n, left_ref, right_ref, w1_ref, w2_ref, disp_ref, conf_ref,
           lt, rt, wb, w2b, tl, tr, te, lfull, rfull, rtail, send_sem, recv_sem):
    rows, feat, width = left_ref.shape
    flat = rows * feat
    col = lax.axis_index("col")
    has_left = col > 0
    has_right = col < n - 1
    left_id = {"col": jnp.maximum(col - 1, 0)}
    right_id = {"col": jnp.minimum(col + 1, n - 1)}
    first = col == 0
    last = col == n - 1

    barrier = pltpu.get_barrier_semaphore()

    @pl.when(has_left)
    def _():
        pl.semaphore_signal(barrier, inc=1, device_id=left_id, device_id_type=MESH)

    @pl.when(has_right)
    def _():
        pl.semaphore_signal(barrier, inc=1, device_id=right_id, device_id_type=MESH)

    left_nat = left_ref[...].reshape(flat, width)
    right_nat = right_ref[...].reshape(flat, width)
    rt[56:56 + width, :] = right_nat.astype(jnp.float32).T
    lt[8:8 + width, :] = left_nat.astype(jnp.float32).T
    rt[64 + width:72 + width, :] = jnp.zeros((8, flat), jnp.float32)

    def copy(index, ref, src, dst, size, target):
        return pltpu.make_async_remote_copy(
            src_ref=ref.at[pl.ds(src, size)], dst_ref=ref.at[pl.ds(dst, size)],
            send_sem=send_sem.at[index], recv_sem=recv_sem.at[index],
            device_id=target, device_id_type=MESH)

    to_right = [copy(0, rt, width, 0, 56, right_id), copy(1, lt, width, 0, 8, right_id)]
    to_left = [copy(2, rt, 56, 56 + width, 8, left_id), copy(3, lt, 8, 8 + width, 8, left_id)]

    pl.semaphore_wait(barrier, has_left.astype(jnp.int32) + has_right.astype(jnp.int32))

    @pl.when(has_right)
    def _():
        for c in to_right:
            c.start()

    @pl.when(has_left)
    def _():
        for c in to_left:
            c.start()

    @pl.when(first)
    def _():
        rt[0:56, :] = jnp.zeros((56, flat), jnp.float32)
        lt[0:8, :] = jnp.zeros((8, flat), jnp.float32)

    @pl.when(last)
    def _():
        rt[56 + width:64 + width, :] = jnp.zeros((8, flat), jnp.float32)
        lt[8 + width:16 + width, :] = jnp.zeros((8, flat), jnp.float32)

    lane = lax.broadcasted_iota(jnp.int32, (32, 128), 1)
    zero = jnp.zeros((32, 32), jnp.float32)
    for a in range(3):
        for e in range(3):
            taps = [w1_ref[a, b, e].astype(jnp.float32) for b in range(3)]
            for side in range(2):
                block = jnp.concatenate([t[:, 32 * side:32 * side + 32] for t in taps] + [zero], axis=1)
                for ro, piece in enumerate(banded(block, lane)):
                    at = a * 128 + ro * 32
                    wb[side, at:at + 32, e * 128:(e + 1) * 128] = piece.astype(jnp.bfloat16)
    lane8 = lax.broadcasted_iota(jnp.int32, (8, 128), 1)
    w2b[...] = jnp.zeros_like(w2b)
    for a in range(3):
        for e in range(3):
            taps = [w2_ref[a, b, e].astype(jnp.float32) for b in range(3)]
            block = jnp.concatenate(taps + [jnp.zeros((1, 32), jnp.float32)], axis=1)
            pieces = banded(jnp.broadcast_to(block, (8, 128)), lane8)
            for di in range(2):
                do = di - (a - 1) + 1
                for ro in range(4):
                    at = e * 16 + do * 4 + ro
                    w2b[at:at + 1, di * 128:(di + 1) * 128] = pieces[ro][0:1, :]

    @pl.when(has_left)
    def _():
        for c in to_right:
            c.wait_recv()

    @pl.when(has_right)
    def _():
        for c in to_left:
            c.wait_recv()

    def taps_of(ref, start, count, side, used):
        lhs = jnp.concatenate(
            [ref[start + e:start + e + count, :].astype(jnp.bfloat16) for e in range(used)], axis=1)
        return lax.dot_general(lhs, wb[side, :, 0:128 * used], NT, preferred_element_type=jnp.float32)

    main = width
    for at, count in ((0, main), (main, 8)):
        res = taps_of(lt, at + 6, count, 0, 3)
        for a in range(3):
            tl[a, at:at + count, :] = res[:, a * 128:(a + 1) * 128]
    res = taps_of(rt, 6, width + 64, 1, 3)
    for a in range(3):
        tr[a, :, :] = res[:, a * 128:(a + 1) * 128]
    res = taps_of(rt, width + 6, 64, 1, 2)
    for a in range(3):
        te[a, :, :] = res[:, a * 128:(a + 1) * 128]

    line = lax.broadcasted_iota(jnp.int32, (width + 8, 128), 0)
    dead = (first & (line == 0)) | (last & (line >= width + 1))
    l_lo = tl[0, :, :]
    l_mid = tl[1, :, :]
    l_hi = tl[2, :, :]
    fill = jnp.full((8, 128), NEG, jnp.float32)
    for k, value in enumerate((l_lo + l_mid + l_hi, l_mid + l_hi, l_lo + l_mid)):
        lfull[k, 0:width + 8, :] = jnp.where(dead, NEG, value)
        lfull[k, width + 8:width + 16, :] = fill
    rfull[...] = tr[0, 2:width + 58, :] + tr[1, 1:width + 57, :] + tr[2, 0:width + 56, :]
    edge = te[0, 2:58, :] + te[1, 1:57, :] + te[2, 0:56, :]
    rtail[0:56, :] = jnp.where(last, edge, rfull[width:width + 56, :])
    rtail[56:64, :] = jnp.zeros((8, 128), jnp.float32)

    def hidden(d):
        s = DISP - 1 - d
        if d == 0:
            k = 1
            body = tr[1, s + 1:s + 1 + width, :] + tr[2, s:s + width, :]
            inner = tr[1, s + 1 + width:s + 17 + width, :] + tr[2, s + width:s + 16 + width, :]
            outer = te[1, s + 1:s + 17, :] + te[2, s:s + 16, :]
            tail = jnp.where(last, outer, inner)
        elif d == DISP - 1:
            k = 2
            body = tr[0, s + 2:s + 2 + width, :] + tr[1, s + 1:s + 1 + width, :]
            inner = tr[0, s + 2 + width:s + 18 + width, :] + tr[1, s + 1 + width:s + 17 + width, :]
            outer = te[0, s + 2:s + 18, :] + te[1, s + 1:s + 17, :]
            tail = jnp.where(last, outer, inner)
        else:
            k = 0
            body = rfull[s:s + width, :]
            tail = rtail[s:s + 16, :]
        body = jnp.maximum(lfull[k, 0:width, :] + body, 0.0).astype(jnp.bfloat16)
        tail = jnp.maximum(lfull[k, width:width + 16, :] + tail, 0.0).astype(jnp.bfloat16)
        return jnp.concatenate([body, tail], axis=0)

    w2 = w2b[...].astype(jnp.bfloat16)
    low = lax.broadcasted_iota(jnp.int32, (8, width), 0) < 4
    total = jnp.zeros((8, width), jnp.float32)
    moment = jnp.zeros((8, width), jnp.float32)
    carry = None
    pairs = DISP // 2
    for k in range(pairs + 1):
        if k < pairs:
            both = jnp.concatenate([hidden(2 * k), hidden(2 * k + 1)], axis=1)
            q = lax.dot_general(w2, both, NT, preferred_element_type=jnp.float32)
            lows = [q[16 * e:16 * e + 8, :] for e in range(3)]
            highs = [q[16 * e + 8:16 * e + 16, :] for e in range(3)]
        if k == 0:
            sums = lows
        elif k == pairs:
            sums = carry
        else:
            sums = [x + y for x, y in zip(lows, carry)]
        carry = highs
        cost = sums[0][:, 0:width] + sums[1][:, 1:width + 1] + sums[2][:, 2:width + 2]
        expo = jnp.exp(-cost)
        if k == 0:
            expo = jnp.where(low, 0.0, expo)
        elif k == pairs:
            expo = jnp.where(low, expo, 0.0)
        total = total + expo
        moment = moment + expo * float(2 * k - 1)
    soft = (moment[0:4, :] + moment[4:8, :] + total[4:8, :]) / (total[0:4, :] + total[4:8, :])
    disp_ref[...] = soft / DISP

    held = jnp.minimum(soft, float(DISP - 1))
    halo = jnp.concatenate([jnp.zeros((8, 128), jnp.float32), rt[0:56, :]], axis=0).T.astype(jnp.bfloat16)
    half = 128
    gap = (lax.broadcasted_iota(jnp.int32, (192, half), 1) - lax.broadcasted_iota(jnp.int32, (192, half), 0) + 64).astype(jnp.float32)
    for r in range(rows):
        band = slice(feat * r, feat * (r + 1))
        for h in range(width // half):
            want = held[r:r + 1, h * half:(h + 1) * half]
            weight = jnp.maximum(0.0, 1.0 - jnp.abs(want - gap))
            head = weight.astype(jnp.bfloat16)
            rest = (weight - head.astype(jnp.float32)).astype(jnp.bfloat16)
            own = right_nat[band, h * half:(h + 1) * half]
            if h == 0:
                before = halo[band, :]
            else:
                before = right_nat[band, (h - 1) * half + 64:h * half]
            warped = jnp.zeros((feat, half), jnp.float32)
            for part in (head, rest):
                warped = warped + jnp.dot(before, part[0:64, :], preferred_element_type=jnp.float32)
                warped = warped + jnp.dot(own, part[64:192, :], preferred_element_type=jnp.float32)
            off = jnp.abs(left_nat[band, h * half:(h + 1) * half].astype(jnp.float32) - warped)
            error = jnp.sum(off, axis=0, keepdims=True) * (1.0 / feat)
            conf_ref[r:r + 1, h * half:(h + 1) * half] = jnp.exp(-error)

    @pl.when(has_right)
    def _():
        for c in to_right:
            c.wait_send()

    @pl.when(has_left)
    def _():
        for c in to_left:
            c.wait_send()


def on_device(left_feat, right_feat, w_first, w_second):
    rows, feat, width = left_feat.shape
    n = lax.axis_size("col")
    f32 = jnp.float32
    vmem = pl.BlockSpec(memory_space=pltpu.VMEM)
    out = jax.ShapeDtypeStruct((rows, width), f32)
    return pl.pallas_call(
        functools.partial(kernel, n),
        out_shape=(out, out),
        in_specs=[vmem] * 4,
        out_specs=(vmem, vmem),
        scratch_shapes=[
            pltpu.VMEM((width + 16, 128), f32),
            pltpu.VMEM((width + 72, 128), f32),
            pltpu.VMEM((2, 384, 384), jnp.bfloat16),
            pltpu.VMEM((48, 256), f32),
            pltpu.VMEM((3, width + 8, 128), f32),
            pltpu.VMEM((3, width + 64, 128), f32),
            pltpu.VMEM((3, 64, 128), f32),
            pltpu.VMEM((3, width + 16, 128), f32),
            pltpu.VMEM((width + 56, 128), f32),
            pltpu.VMEM((64, 128), f32),
            pltpu.SemaphoreType.DMA((4,)),
            pltpu.SemaphoreType.DMA((4,)),
        ],
        compiler_params=pltpu.CompilerParams(
            collective_id=0, has_side_effects=True, vmem_limit_bytes=32 << 20),
    )(left_feat, right_feat, w_first, w_second)


def solution(mesh):
    in_specs = (P("band", None, "col"), P("band", None, "col"), P(), P())
    out_specs = (P("band", "col"), P("band", "col"))
    return jax.shard_map(
        on_device, mesh=mesh, in_specs=in_specs, out_specs=out_specs, check_vma=False
    )
```

```python
import functools

import jax
import jax.numpy as jnp
from jax import lax
from jax.experimental import pallas as pl
from jax.experimental.pallas import tpu as pltpu
from jax.sharding import PartitionSpec as P

DISP = 48
NEG = -1e30
NT = (((1,), (1,)), ((), ()))
MESH = pl.DeviceIdType.MESH


def banded(block, lane):
    return [
        jnp.where(lane < 64, pltpu.roll(block, 96, 1), 0.0),
        block,
        pltpu.roll(block, 32, 1),
        jnp.where(lane >= 64, pltpu.roll(block, 64, 1), 0.0),
    ]


def tables_kernel(n, left_hbm, right_hbm, w1_hbm, w2_hbm,
                  left_out, right_out, lfull, rfull, rtail, ends, w2b, halo_out,
                  lt, rt, wb, tl, tr, te, w1_ref, w2_ref, load_sem, send_sem, recv_sem):
    rows, feat, width = left_out.shape
    flat = rows * feat
    f32, bf16 = jnp.float32, jnp.bfloat16
    col = lax.axis_index("col")
    has_left = col > 0
    has_right = col < n - 1
    left_id = {"col": jnp.maximum(col - 1, 0)}
    right_id = {"col": jnp.minimum(col + 1, n - 1)}
    first = col == 0
    last = col == n - 1

    barrier = pltpu.get_barrier_semaphore()

    @pl.when(has_left)
    def _():
        pl.semaphore_signal(barrier, inc=1, device_id=left_id, device_id_type=MESH)

    @pl.when(has_right)
    def _():
        pl.semaphore_signal(barrier, inc=1, device_id=right_id, device_id_type=MESH)

    loads = [
        pltpu.make_async_copy(src, dst, load_sem.at[i])
        for i, (src, dst) in enumerate(
            ((right_hbm, right_out), (left_hbm, left_out), (w1_hbm, w1_ref), (w2_hbm, w2_ref)))
    ]
    for c in loads:
        c.start()

    rt[64 + width:72 + width, :] = jnp.zeros((8, flat), f32)

    @pl.when(first)
    def _():
        rt[0:56, :] = jnp.zeros((56, flat), f32)
        lt[0:8, :] = jnp.zeros((8, flat), f32)

    @pl.when(last)
    def _():
        rt[56 + width:64 + width, :] = jnp.zeros((8, flat), f32)
        lt[8 + width:16 + width, :] = jnp.zeros((8, flat), f32)

    w2b[...] = jnp.zeros_like(w2b)

    loads[0].wait()
    rt[56:56 + width, :] = right_out[...].reshape(flat, width).astype(f32).T
    loads[1].wait()
    lt[8:8 + width, :] = left_out[...].reshape(flat, width).astype(f32).T

    def copy(index, ref, src, dst, size, target):
        return pltpu.make_async_remote_copy(
            src_ref=ref.at[pl.ds(src, size)], dst_ref=ref.at[pl.ds(dst, size)],
            send_sem=send_sem.at[index], recv_sem=recv_sem.at[index],
            device_id=target, device_id_type=MESH)

    to_right = [copy(0, rt, width, 0, 56, right_id), copy(1, lt, width, 0, 8, right_id)]
    to_left = [copy(2, rt, 56, 56 + width, 8, left_id), copy(3, lt, 8, 8 + width, 8, left_id)]

    pl.semaphore_wait(barrier, has_left.astype(jnp.int32) + has_right.astype(jnp.int32))

    @pl.when(has_right)
    def _():
        for c in to_right:
            c.start()

    @pl.when(has_left)
    def _():
        for c in to_left:
            c.start()

    loads[2].wait()
    lane = lax.broadcasted_iota(jnp.int32, (32, 128), 1)
    zero = jnp.zeros((32, 32), f32)
    for a in range(3):
        for e in range(3):
            taps = [w1_ref[a, b, e].astype(f32) for b in range(3)]
            for side in range(2):
                block = jnp.concatenate([t[:, 32 * side:32 * side + 32] for t in taps] + [zero], axis=1)
                for ro, piece in enumerate(banded(block, lane)):
                    at = a * 128 + ro * 32
                    wb[side, at:at + 32, e * 128:(e + 1) * 128] = piece.astype(bf16)

    def taps_of(ref, start, count, side, used):
        lhs = jnp.concatenate(
            [ref[start + e:start + e + count, :].astype(bf16) for e in range(used)], axis=1)
        return lax.dot_general(lhs, wb[side, :, 0:128 * used], NT, preferred_element_type=f32)

    def fill(out, ref, at, count, side):
        res = taps_of(ref, at + 6, count, side, 3)
        for a in range(3):
            out[a, at:at + count, :] = res[:, a * 128:(a + 1) * 128]

    fill(tl, lt, 8, width - 8, 0)
    fill(tr, rt, 56, width - 8, 1)

    loads[3].wait()
    lane8 = lax.broadcasted_iota(jnp.int32, (8, 128), 1)
    for a in range(3):
        for e in range(3):
            taps = [w2_ref[a, b, e:e + 1, :].astype(f32) for b in range(3)]
            block = jnp.concatenate(taps + [jnp.zeros((1, 32), f32)], axis=1)
            pieces = banded(jnp.broadcast_to(block, (8, 128)), lane8)
            for di in range(2):
                do = di - (a - 1) + 1
                for ro in range(4):
                    at = e * 16 + do * 4 + ro
                    w2b[at:at + 1, di * 128:(di + 1) * 128] = pieces[ro][0:1, :]

    @pl.when(has_left)
    def _():
        for c in to_right:
            c.wait_recv()

    @pl.when(has_right)
    def _():
        for c in to_left:
            c.wait_recv()

    fill(tl, lt, 0, 8, 0)
    fill(tl, lt, width, 8, 0)
    fill(tr, rt, 0, 56, 1)
    fill(tr, rt, width + 48, 16, 1)
    res = taps_of(rt, width + 6, 64, 1, 2)
    for a in range(3):
        te[a, :, :] = res[:, a * 128:(a + 1) * 128]
    halo_out[...] = jnp.concatenate([jnp.zeros((8, 128), f32), rt[0:56, :]], axis=0).T.astype(bf16)

    line = lax.broadcasted_iota(jnp.int32, (width + 8, 128), 0)
    dead = (first & (line == 0)) | (last & (line >= width + 1))
    l_lo = tl[0, :, :]
    l_mid = tl[1, :, :]
    l_hi = tl[2, :, :]
    lfull[0:width + 8, :] = jnp.where(dead, NEG, l_lo + l_mid + l_hi)
    lfull[width + 8:width + 16, :] = jnp.full((8, 128), NEG, f32)
    rfull[...] = tr[0, 2:width + 58, :] + tr[1, 1:width + 57, :] + tr[2, 0:width + 56, :]
    edge = te[0, 2:58, :] + te[1, 1:57, :] + te[2, 0:56, :]
    rtail[0:56, :] = jnp.where(last, edge, rfull[width:width + 56, :])
    rtail[56:64, :] = jnp.zeros((8, 128), f32)

    for k, (value, a, s) in enumerate(((l_mid + l_hi, 1, DISP - 1), (l_lo + l_mid, 0, 1))):
        value = jnp.where(dead, NEG, value)
        body = tr[a, s + 1:s + 1 + width, :] + tr[a + 1, s:s + width, :]
        inner = tr[a, s + 1 + width:s + 9 + width, :] + tr[a + 1, s + width:s + 8 + width, :]
        outer = te[a, s + 1:s + 9, :] + te[a + 1, s:s + 8, :]
        tail = jnp.where(last, outer, inner)
        body = jnp.maximum(value[0:width] + body, 0.0)
        tail = jnp.maximum(value[width:width + 8] + tail, 0.0)
        ends[k, 0:width, :] = body.astype(bf16)
        ends[k, width:width + 16, :] = jnp.concatenate([tail, jnp.zeros((8, 128), f32)], axis=0).astype(bf16)

    @pl.when(has_right)
    def _():
        for c in to_right:
            c.wait_send()

    @pl.when(has_left)
    def _():
        for c in to_left:
            c.wait_send()


def cost_kernel(left_ref, right_ref, lfull, rfull, rtail, ends, w2b, halo_ref,
                disp_hbm, conf_hbm, disp_ref, conf_ref, sem):
    rows, feat, width = left_ref.shape
    flat = rows * feat
    f32, bf16 = jnp.float32, jnp.bfloat16

    def hidden(d):
        if d == 0:
            return ends[0]
        if d == DISP - 1:
            return ends[1]
        s = DISP - 1 - d
        body = jnp.maximum(lfull[0:width, :] + rfull[s:s + width, :], 0.0).astype(bf16)
        tail = jnp.maximum(lfull[width:width + 16, :] + rtail[s:s + 16, :], 0.0).astype(bf16)
        return jnp.concatenate([body, tail], axis=0)

    w2 = w2b[...].astype(jnp.bfloat16)
    low = lax.broadcasted_iota(jnp.int32, (8, width), 0) < 4
    total = jnp.zeros((8, width), jnp.float32)
    moment = jnp.zeros((8, width), jnp.float32)
    carry = None
    pairs = DISP // 2
    for k in range(pairs + 1):
        if k < pairs:
            both = jnp.concatenate([hidden(2 * k), hidden(2 * k + 1)], axis=1)
            q = lax.dot_general(w2, both, NT, preferred_element_type=jnp.float32)
            lows = [q[16 * e:16 * e + 8, :] for e in range(3)]
            highs = [q[16 * e + 8:16 * e + 16, :] for e in range(3)]
        if k == 0:
            sums = lows
        elif k == pairs:
            sums = carry
        else:
            sums = [x + y for x, y in zip(lows, carry)]
        carry = highs
        cost = sums[0][:, 0:width] + sums[1][:, 1:width + 1] + sums[2][:, 2:width + 2]
        expo = jnp.exp(-cost)
        if k == 0:
            expo = jnp.where(low, 0.0, expo)
        elif k == pairs:
            expo = jnp.where(low, expo, 0.0)
        total = total + expo
        moment = moment + expo * float(2 * k - 1)
    soft = (moment[0:4, :] + moment[4:8, :] + total[4:8, :]) / (total[0:4, :] + total[4:8, :])
    disp_ref[...] = soft / DISP
    save_disp = pltpu.make_async_copy(disp_ref, disp_hbm, sem.at[0])
    save_disp.start()

    held = jnp.minimum(soft, float(DISP - 1))
    halo = halo_ref[...]
    left_nat = left_ref[...].reshape(flat, width)
    right_nat = right_ref[...].reshape(flat, width)
    half = 128
    gap = (lax.broadcasted_iota(jnp.int32, (192, half), 1) - lax.broadcasted_iota(jnp.int32, (192, half), 0) + 64).astype(jnp.float32)
    for r in range(rows):
        band = slice(feat * r, feat * (r + 1))
        for h in range(width // half):
            want = held[r:r + 1, h * half:(h + 1) * half]
            weight = jnp.maximum(0.0, 1.0 - jnp.abs(want - gap))
            head = weight.astype(jnp.bfloat16)
            rest = (weight - head.astype(jnp.float32)).astype(jnp.bfloat16)
            own = right_nat[band, h * half:(h + 1) * half]
            if h == 0:
                before = halo[band, :]
            else:
                before = right_nat[band, (h - 1) * half + 64:h * half]
            warped = jnp.zeros((feat, half), jnp.float32)
            for part in (head, rest):
                warped = warped + jnp.dot(before, part[0:64, :], preferred_element_type=jnp.float32)
                warped = warped + jnp.dot(own, part[64:192, :], preferred_element_type=jnp.float32)
            off = jnp.abs(left_nat[band, h * half:(h + 1) * half].astype(jnp.float32) - warped)
            error = jnp.sum(off, axis=0, keepdims=True) * (1.0 / feat)
            conf_ref[r:r + 1, h * half:(h + 1) * half] = jnp.exp(-error)
    save_conf = pltpu.make_async_copy(conf_ref, conf_hbm, sem.at[1])
    save_conf.start()
    save_disp.wait()
    save_conf.wait()


def on_device(left_feat, right_feat, w_first, w_second):
    rows, feat, width = left_feat.shape
    n = lax.axis_size("col")
    f32, bf16 = jnp.float32, jnp.bfloat16
    w_cost = w_second[:, :, :, 0, :]
    vmem = pl.BlockSpec(memory_space=pltpu.VMEM)
    hbm = pl.BlockSpec(memory_space=pltpu.HBM)
    shape = jax.ShapeDtypeStruct
    tables = pl.pallas_call(
        functools.partial(tables_kernel, n),
        out_shape=(
            shape(left_feat.shape, bf16),
            shape(right_feat.shape, bf16),
            shape((width + 16, 128), f32),
            shape((width + 56, 128), f32),
            shape((64, 128), f32),
            shape((2, width + 16, 128), bf16),
            shape((48, 256), f32),
            shape((128, 64), bf16),
        ),
        in_specs=[hbm] * 4,
        out_specs=(vmem,) * 8,
        scratch_shapes=[
            pltpu.VMEM((width + 16, 128), f32),
            pltpu.VMEM((width + 72, 128), f32),
            pltpu.VMEM((2, 384, 384), bf16),
            pltpu.VMEM((3, width + 8, 128), f32),
            pltpu.VMEM((3, width + 64, 128), f32),
            pltpu.VMEM((3, 64, 128), f32),
            pltpu.VMEM(w_first.shape, bf16),
            pltpu.VMEM(w_cost.shape, bf16),
            pltpu.SemaphoreType.DMA((4,)),
            pltpu.SemaphoreType.DMA((4,)),
            pltpu.SemaphoreType.DMA((4,)),
        ],
        compiler_params=pltpu.CompilerParams(
            collective_id=0, has_side_effects=True, vmem_limit_bytes=16 << 20),
    )(*(pltpu.with_memory_space_constraint(x, pltpu.HBM) for x in (left_feat, right_feat, w_first, w_cost)))
    out = shape((rows, width), f32)
    return pl.pallas_call(
        cost_kernel,
        out_shape=(out, out),
        in_specs=[vmem] * 8,
        out_specs=(hbm, hbm),
        scratch_shapes=[
            pltpu.VMEM((rows, width), f32),
            pltpu.VMEM((rows, width), f32),
            pltpu.SemaphoreType.DMA((2,)),
        ],
        compiler_params=pltpu.CompilerParams(vmem_limit_bytes=16 << 20),
    )(*tables)


def solution(mesh):
    in_specs = (P("band", None, "col"), P("band", None, "col"), P(), P())
    out_specs = (P("band", "col"), P("band", "col"))
    return jax.shard_map(
        on_device, mesh=mesh, in_specs=in_specs, out_specs=out_specs, check_vma=False
    )
```

```python
import functools

import jax
import jax.numpy as jnp
from jax import lax
from jax.experimental import pallas as pl
from jax.experimental.pallas import tpu as pltpu
from jax.sharding import PartitionSpec as P

DISP = 48
NEG = -1e30
NT = (((1,), (1,)), ((), ()))
MESH = pl.DeviceIdType.MESH


def banded(block, lane):
    return [
        jnp.where(lane < 64, pltpu.roll(block, 96, 1), 0.0),
        block,
        pltpu.roll(block, 32, 1),
        jnp.where(lane >= 64, pltpu.roll(block, 64, 1), 0.0),
    ]


def tables_kernel(n, left_hbm, right_hbm, w1_hbm, w2_hbm,
                  left_out, right_out, lfull, rfull, rtail, ends, w2b, halo_out,
                  lt, rt, wb, tl, tr, te, w1_ref, w2_ref, out_r, out_l, in_l, in_r, load_sem, send_sem, recv_sem):
    rows, feat, width = left_out.shape
    flat = rows * feat
    f32, bf16 = jnp.float32, jnp.bfloat16
    col = lax.axis_index("col")
    has_left = col > 0
    has_right = col < n - 1
    left_id = {"col": jnp.maximum(col - 1, 0)}
    right_id = {"col": jnp.minimum(col + 1, n - 1)}
    first = col == 0
    last = col == n - 1

    barrier = pltpu.get_barrier_semaphore()

    @pl.when(has_left)
    def _():
        pl.semaphore_signal(barrier, inc=1, device_id=left_id, device_id_type=MESH)

    @pl.when(has_right)
    def _():
        pl.semaphore_signal(barrier, inc=1, device_id=right_id, device_id_type=MESH)

    loads = [
        pltpu.make_async_copy(src, dst, load_sem.at[i])
        for i, (src, dst) in enumerate(
            ((right_hbm, right_out), (left_hbm, left_out), (w1_hbm, w1_ref), (w2_hbm, w2_ref)))
    ]
    for c in loads:
        c.start()

    rt[64 + width:72 + width, :] = jnp.zeros((8, flat), f32)

    @pl.when(first)
    def _():
        rt[0:56, :] = jnp.zeros((56, flat), f32)
        lt[0:8, :] = jnp.zeros((8, flat), f32)

    @pl.when(last)
    def _():
        rt[56 + width:64 + width, :] = jnp.zeros((8, flat), f32)
        lt[8 + width:16 + width, :] = jnp.zeros((8, flat), f32)

    w2b[...] = jnp.zeros_like(w2b)

    loads[0].wait()
    rt[56:56 + width, :] = right_out[...].reshape(flat, width).astype(f32).T
    loads[1].wait()
    lt[8:8 + width, :] = left_out[...].reshape(flat, width).astype(f32).T

    out_r[0:64, :] = rt[width - 8:width + 56, :].astype(bf16)
    out_r[64:80, :] = lt[width - 8:width + 8, :].astype(bf16)
    out_l[0:16, :] = rt[56:72, :].astype(bf16)
    out_l[16:32, :] = lt[8:24, :].astype(bf16)

    def copy(index, src, dst, target):
        return pltpu.make_async_remote_copy(
            src_ref=src, dst_ref=dst, send_sem=send_sem.at[index], recv_sem=recv_sem.at[index],
            device_id=target, device_id_type=MESH)

    to_right = copy(0, out_r, in_l, right_id)
    to_left = copy(1, out_l, in_r, left_id)

    pl.semaphore_wait(barrier, has_left.astype(jnp.int32) + has_right.astype(jnp.int32))

    @pl.when(has_right)
    def _():
        to_right.start()

    @pl.when(has_left)
    def _():
        to_left.start()

    loads[2].wait()
    lane = lax.broadcasted_iota(jnp.int32, (32, 128), 1)
    zero = jnp.zeros((32, 32), f32)
    for a in range(3):
        for e in range(3):
            taps = [w1_ref[a, b, e].astype(f32) for b in range(3)]
            for side in range(2):
                block = jnp.concatenate([t[:, 32 * side:32 * side + 32] for t in taps] + [zero], axis=1)
                for ro, piece in enumerate(banded(block, lane)):
                    at = a * 128 + ro * 32
                    wb[side, at:at + 32, e * 128:(e + 1) * 128] = piece.astype(bf16)

    def shifted(ref, start, count, used=3):
        parts = [ref[start + e:start + e + count, :].astype(bf16) for e in range(used)]
        return jnp.concatenate(parts + [jnp.zeros((count, 128), bf16)] * (3 - used), axis=1)

    def fill(side, pieces):
        lhs = [shifted(ref, start, count, used) for ref, start, count, used, _, _ in pieces]
        lhs = lhs[0] if len(lhs) == 1 else jnp.concatenate(lhs, axis=0)
        res = lax.dot_general(lhs, wb[side], NT, preferred_element_type=f32)
        at = 0
        for _, _, count, _, out, to in pieces:
            for a in range(3):
                out[a, to:to + count, :] = res[at:at + count, a * 128:(a + 1) * 128]
            at += count

    def left_table(taps, lo, hi):
        value = sum(tl[a, lo:hi, :] for a in taps)
        line = lo + lax.broadcasted_iota(jnp.int32, (hi - lo, 128), 0)
        dead = (first & (line == 0)) | (last & (line >= width + 1))
        return jnp.where(dead, NEG, value)

    def right_table(lo, hi):
        rfull[lo:hi, :] = tr[0, lo + 2:hi + 2, :] + tr[1, lo + 1:hi + 1, :] + tr[2, lo:hi, :]

    end_taps = ((1, 2, DISP - 1), (0, 1, 1))

    def end_rows(k, lo, hi):
        a, b, s = end_taps[k]
        body = tr[a, s + 1 + lo:s + 1 + hi, :] + tr[b, s + lo:s + hi, :]
        ends[k, lo:hi, :] = jnp.maximum(left_table((a, b), lo, hi) + body, 0.0).astype(bf16)

    fill(0, [(lt, 14, width - 8, 3, tl, 8)])
    fill(1, [(rt, 62, width - 8, 3, tr, 56)])
    lfull[8:width, :] = left_table((0, 1, 2), 8, width)
    right_table(56, width + 40)
    end_rows(0, 16, width - 16)
    end_rows(1, 64, width - 16)

    loads[3].wait()
    lane8 = lax.broadcasted_iota(jnp.int32, (8, 128), 1)
    for a in range(3):
        for e in range(3):
            taps = [w2_ref[a, b, e:e + 1, :].astype(f32) for b in range(3)]
            block = jnp.concatenate(taps + [jnp.zeros((1, 32), f32)], axis=1)
            pieces = banded(jnp.broadcast_to(block, (8, 128)), lane8)
            for di in range(2):
                do = di - (a - 1) + 1
                for ro in range(4):
                    at = e * 16 + do * 4 + ro
                    w2b[at:at + 1, di * 128:(di + 1) * 128] = pieces[ro][0:1, :]

    @pl.when(has_left)
    def _():
        to_right.wait_recv()
        rt[0:56, :] = in_l[8:64, :].astype(f32)
        lt[0:8, :] = in_l[72:80, :].astype(f32)

    @pl.when(has_right)
    def _():
        to_left.wait_recv()
        rt[56 + width:64 + width, :] = in_r[0:8, :].astype(f32)
        lt[8 + width:16 + width, :] = in_r[16:24, :].astype(f32)

    fill(1, [(rt, 6, 56, 3, tr, 0), (rt, width + 54, 16, 3, tr, width + 48), (rt, width + 6, 64, 2, te, 0)])
    fill(0, [(lt, 6, 8, 3, tl, 0), (lt, width + 6, 8, 3, tl, width)])
    halo_out[...] = jnp.concatenate([jnp.zeros((8, 128), f32), rt[0:56, :]], axis=0).T.astype(bf16)

    lfull[0:8, :] = left_table((0, 1, 2), 0, 8)
    lfull[width:width + 8, :] = left_table((0, 1, 2), width, width + 8)
    lfull[width + 8:width + 16, :] = jnp.full((8, 128), NEG, f32)
    right_table(0, 56)
    right_table(width + 40, width + 56)
    edge = te[0, 2:58, :] + te[1, 1:57, :] + te[2, 0:56, :]
    rtail[0:56, :] = jnp.where(last, edge, rfull[width:width + 56, :])
    rtail[56:64, :] = jnp.zeros((8, 128), f32)
    end_rows(0, 0, 16)
    end_rows(0, width - 16, width)
    end_rows(1, 0, 64)
    end_rows(1, width - 16, width)
    for k, (a, b, s) in enumerate(end_taps):
        inner = tr[a, s + 1 + width:s + 9 + width, :] + tr[b, s + width:s + 8 + width, :]
        outer = te[a, s + 1:s + 9, :] + te[b, s:s + 8, :]
        tail = jnp.maximum(left_table((a, b), width, width + 8) + jnp.where(last, outer, inner), 0.0)
        ends[k, width:width + 16, :] = jnp.concatenate([tail, jnp.zeros((8, 128), f32)], axis=0).astype(bf16)

    @pl.when(has_right)
    def _():
        to_right.wait_send()

    @pl.when(has_left)
    def _():
        to_left.wait_send()


def cost_kernel(left_ref, right_ref, lfull, rfull, rtail, ends, w2b, halo_ref,
                disp_hbm, conf_hbm, disp_ref, conf_ref, sem):
    rows, feat, width = left_ref.shape
    flat = rows * feat
    f32, bf16 = jnp.float32, jnp.bfloat16

    def hidden(d):
        if d == 0:
            return ends[0]
        if d == DISP - 1:
            return ends[1]
        s = DISP - 1 - d
        body = jnp.maximum(lfull[0:width, :] + rfull[s:s + width, :], 0.0).astype(bf16)
        tail = jnp.maximum(lfull[width:width + 16, :] + rtail[s:s + 16, :], 0.0).astype(bf16)
        return jnp.concatenate([body, tail], axis=0)

    w2 = w2b[...].astype(jnp.bfloat16)
    low = lax.broadcasted_iota(jnp.int32, (8, width), 0) < 4
    total = jnp.zeros((8, width), jnp.float32)
    moment = jnp.zeros((8, width), jnp.float32)
    carry = None
    pairs = DISP // 2
    for k in range(pairs + 1):
        if k < pairs:
            both = jnp.concatenate([hidden(2 * k), hidden(2 * k + 1)], axis=1)
            q = lax.dot_general(w2, both, NT, preferred_element_type=jnp.float32)
            lows = [q[16 * e:16 * e + 8, :] for e in range(3)]
            highs = [q[16 * e + 8:16 * e + 16, :] for e in range(3)]
        if k == 0:
            sums = lows
        elif k == pairs:
            sums = carry
        else:
            sums = [x + y for x, y in zip(lows, carry)]
        carry = highs
        cost = sums[0][:, 0:width] + sums[1][:, 1:width + 1] + sums[2][:, 2:width + 2]
        expo = jnp.exp(-cost)
        if k == 0:
            expo = jnp.where(low, 0.0, expo)
        elif k == pairs:
            expo = jnp.where(low, expo, 0.0)
        total = total + expo
        moment = moment + expo * float(2 * k - 1)
    soft = (moment[0:4, :] + moment[4:8, :] + total[4:8, :]) / (total[0:4, :] + total[4:8, :])
    disp_ref[...] = soft / DISP
    save_disp = pltpu.make_async_copy(disp_ref, disp_hbm, sem.at[0])
    save_disp.start()

    held = jnp.minimum(soft, float(DISP - 1))
    halo = halo_ref[...]
    left_nat = left_ref[...].reshape(flat, width)
    right_nat = right_ref[...].reshape(flat, width)
    half = 128
    gap = (lax.broadcasted_iota(jnp.int32, (192, half), 1) - lax.broadcasted_iota(jnp.int32, (192, half), 0) + 64).astype(jnp.float32)
    for r in range(rows):
        band = slice(feat * r, feat * (r + 1))
        for h in range(width // half):
            want = held[r:r + 1, h * half:(h + 1) * half]
            weight = jnp.maximum(0.0, 1.0 - jnp.abs(want - gap))
            head = weight.astype(jnp.bfloat16)
            rest = (weight - head.astype(jnp.float32)).astype(jnp.bfloat16)
            own = right_nat[band, h * half:(h + 1) * half]
            if h == 0:
                before = halo[band, :]
            else:
                before = right_nat[band, (h - 1) * half + 64:h * half]
            warped = jnp.zeros((feat, half), jnp.float32)
            for part in (head, rest):
                warped = warped + jnp.dot(before, part[0:64, :], preferred_element_type=jnp.float32)
                warped = warped + jnp.dot(own, part[64:192, :], preferred_element_type=jnp.float32)
            off = jnp.abs(left_nat[band, h * half:(h + 1) * half].astype(jnp.float32) - warped)
            error = jnp.sum(off, axis=0, keepdims=True) * (1.0 / feat)
            conf_ref[r:r + 1, h * half:(h + 1) * half] = jnp.exp(-error)
    save_conf = pltpu.make_async_copy(conf_ref, conf_hbm, sem.at[1])
    save_conf.start()
    save_disp.wait()
    save_conf.wait()


def on_device(left_feat, right_feat, w_first, w_second):
    rows, feat, width = left_feat.shape
    n = lax.axis_size("col")
    f32, bf16 = jnp.float32, jnp.bfloat16
    w_cost = w_second[:, :, :, 0, :]
    vmem = pl.BlockSpec(memory_space=pltpu.VMEM)
    hbm = pl.BlockSpec(memory_space=pltpu.HBM)
    shape = jax.ShapeDtypeStruct
    tables = pl.pallas_call(
        functools.partial(tables_kernel, n),
        out_shape=(
            shape(left_feat.shape, bf16),
            shape(right_feat.shape, bf16),
            shape((width + 16, 128), f32),
            shape((width + 56, 128), f32),
            shape((64, 128), f32),
            shape((2, width + 16, 128), bf16),
            shape((48, 256), f32),
            shape((128, 64), bf16),
        ),
        in_specs=[hbm] * 4,
        out_specs=(vmem,) * 8,
        scratch_shapes=[
            pltpu.VMEM((width + 16, 128), f32),
            pltpu.VMEM((width + 72, 128), f32),
            pltpu.VMEM((2, 384, 384), bf16),
            pltpu.VMEM((3, width + 8, 128), f32),
            pltpu.VMEM((3, width + 64, 128), f32),
            pltpu.VMEM((3, 64, 128), f32),
            pltpu.VMEM(w_first.shape, bf16),
            pltpu.VMEM(w_cost.shape, bf16),
            pltpu.VMEM((80, 128), bf16),
            pltpu.VMEM((32, 128), bf16),
            pltpu.VMEM((80, 128), bf16),
            pltpu.VMEM((32, 128), bf16),
            pltpu.SemaphoreType.DMA((4,)),
            pltpu.SemaphoreType.DMA((2,)),
            pltpu.SemaphoreType.DMA((2,)),
        ],
        compiler_params=pltpu.CompilerParams(
            collective_id=0, has_side_effects=True, vmem_limit_bytes=16 << 20),
    )(*(pltpu.with_memory_space_constraint(x, pltpu.HBM) for x in (left_feat, right_feat, w_first, w_cost)))
    out = shape((rows, width), f32)
    return pl.pallas_call(
        cost_kernel,
        out_shape=(out, out),
        in_specs=[vmem] * 8,
        out_specs=(hbm, hbm),
        scratch_shapes=[
            pltpu.VMEM((rows, width), f32),
            pltpu.VMEM((rows, width), f32),
            pltpu.SemaphoreType.DMA((2,)),
        ],
        compiler_params=pltpu.CompilerParams(vmem_limit_bytes=16 << 20),
    )(*tables)


def solution(mesh):
    in_specs = (P("band", None, "col"), P("band", None, "col"), P(), P())
    out_specs = (P("band", "col"), P("band", "col"))
    return jax.shard_map(
        on_device, mesh=mesh, in_specs=in_specs, out_specs=out_specs, check_vma=False
    )
```

```python
import functools

import jax
import jax.numpy as jnp
from jax import lax
from jax.experimental import pallas as pl
from jax.experimental.pallas import tpu as pltpu
from jax.sharding import PartitionSpec as P

DISP = 48
NEG = -1e30
NT = (((1,), (1,)), ((), ()))
MESH = pl.DeviceIdType.MESH


def banded(block, lane):
    return [
        jnp.where(lane < 64, pltpu.roll(block, 96, 1), 0.0),
        block,
        pltpu.roll(block, 32, 1),
        jnp.where(lane >= 64, pltpu.roll(block, 64, 1), 0.0),
    ]


def cost_sums(weights, hidden):
    carry = None
    pairs = DISP // 2
    for k in range(pairs + 1):
        if k < pairs:
            both = jnp.concatenate([hidden(2 * k), hidden(2 * k + 1)], axis=1)
            q = lax.dot_general(weights, both, NT, preferred_element_type=jnp.float32)
            lows = [q[16 * e:16 * e + 8, :] for e in range(3)]
            highs = [q[16 * e + 8:16 * e + 16, :] for e in range(3)]
        if k == 0:
            sums = lows
        elif k == pairs:
            sums = carry
        else:
            sums = [x + y for x, y in zip(lows, carry)]
        carry = highs
        yield k, sums


def tables_kernel(n, left_hbm, right_hbm, w1_hbm, w2_hbm,
                  left_out, right_out, lfull, rfull, rtail, ends, w2b, halo_out, costs,
                  lt, rt, wb, tl, tr, te, w1_ref, w2_ref, out_r, out_l, in_l, in_r, load_sem, send_sem, recv_sem):
    rows, feat, width = left_out.shape
    flat = rows * feat
    f32, bf16 = jnp.float32, jnp.bfloat16
    col = lax.axis_index("col")
    has_left = col > 0
    has_right = col < n - 1
    left_id = {"col": jnp.maximum(col - 1, 0)}
    right_id = {"col": jnp.minimum(col + 1, n - 1)}
    first = col == 0
    last = col == n - 1

    barrier = pltpu.get_barrier_semaphore()

    @pl.when(has_left)
    def _():
        pl.semaphore_signal(barrier, inc=1, device_id=left_id, device_id_type=MESH)

    @pl.when(has_right)
    def _():
        pl.semaphore_signal(barrier, inc=1, device_id=right_id, device_id_type=MESH)

    loads = [
        pltpu.make_async_copy(src, dst, load_sem.at[i])
        for i, (src, dst) in enumerate(
            ((right_hbm, right_out), (left_hbm, left_out), (w1_hbm, w1_ref), (w2_hbm, w2_ref)))
    ]
    for c in loads:
        c.start()

    rt[64 + width:72 + width, :] = jnp.zeros((8, flat), f32)

    @pl.when(first)
    def _():
        rt[0:56, :] = jnp.zeros((56, flat), f32)
        lt[0:8, :] = jnp.zeros((8, flat), f32)

    @pl.when(last)
    def _():
        rt[56 + width:64 + width, :] = jnp.zeros((8, flat), f32)
        lt[8 + width:16 + width, :] = jnp.zeros((8, flat), f32)

    w2b[...] = jnp.zeros_like(w2b)

    loads[0].wait()
    rt[56:56 + width, :] = right_out[...].reshape(flat, width).astype(f32).T
    loads[1].wait()
    lt[8:8 + width, :] = left_out[...].reshape(flat, width).astype(f32).T

    out_r[0:64, :] = rt[width - 8:width + 56, :].astype(bf16)
    out_r[64:80, :] = lt[width - 8:width + 8, :].astype(bf16)
    out_l[0:16, :] = rt[56:72, :].astype(bf16)
    out_l[16:32, :] = lt[8:24, :].astype(bf16)

    def copy(index, src, dst, target):
        return pltpu.make_async_remote_copy(
            src_ref=src, dst_ref=dst, send_sem=send_sem.at[index], recv_sem=recv_sem.at[index],
            device_id=target, device_id_type=MESH)

    to_right = copy(0, out_r, in_l, right_id)
    to_left = copy(1, out_l, in_r, left_id)

    pl.semaphore_wait(barrier, has_left.astype(jnp.int32) + has_right.astype(jnp.int32))

    @pl.when(has_right)
    def _():
        to_right.start()

    @pl.when(has_left)
    def _():
        to_left.start()

    loads[2].wait()
    lane = lax.broadcasted_iota(jnp.int32, (32, 128), 1)
    zero = jnp.zeros((32, 32), f32)
    for a in range(3):
        for e in range(3):
            taps = [w1_ref[a, b, e].astype(f32) for b in range(3)]
            for side in range(2):
                block = jnp.concatenate([t[:, 32 * side:32 * side + 32] for t in taps] + [zero], axis=1)
                for ro, piece in enumerate(banded(block, lane)):
                    at = a * 128 + ro * 32
                    wb[side, at:at + 32, e * 128:(e + 1) * 128] = piece.astype(bf16)

    def shifted(ref, start, count, used=3):
        parts = [ref[start + e:start + e + count, :].astype(bf16) for e in range(used)]
        return jnp.concatenate(parts + [jnp.zeros((count, 128), bf16)] * (3 - used), axis=1)

    def fill(side, pieces):
        lhs = [shifted(ref, start, count, used) for ref, start, count, used, _, _ in pieces]
        lhs = lhs[0] if len(lhs) == 1 else jnp.concatenate(lhs, axis=0)
        res = lax.dot_general(lhs, wb[side], NT, preferred_element_type=f32)
        at = 0
        for _, _, count, _, out, to in pieces:
            for a in range(3):
                out[a, to:to + count, :] = res[at:at + count, a * 128:(a + 1) * 128]
            at += count

    def left_table(taps, lo, hi):
        value = sum(tl[a, lo:hi, :] for a in taps)
        line = lo + lax.broadcasted_iota(jnp.int32, (hi - lo, 128), 0)
        dead = (first & (line == 0)) | (last & (line >= width + 1))
        return jnp.where(dead, NEG, value)

    def right_table(lo, hi):
        rfull[lo:hi, :] = tr[0, lo + 2:hi + 2, :] + tr[1, lo + 1:hi + 1, :] + tr[2, lo:hi, :]

    end_taps = ((1, 2, DISP - 1), (0, 1, 1))

    def end_rows(k, lo, hi):
        a, b, s = end_taps[k]
        body = tr[a, s + 1 + lo:s + 1 + hi, :] + tr[b, s + lo:s + hi, :]
        ends[k, lo:hi, :] = jnp.maximum(left_table((a, b), lo, hi) + body, 0.0).astype(bf16)

    loads[3].wait()
    lane8 = lax.broadcasted_iota(jnp.int32, (8, 128), 1)
    for a in range(3):
        for e in range(3):
            taps = [w2_ref[a, b, e:e + 1, :].astype(f32) for b in range(3)]
            block = jnp.concatenate(taps + [jnp.zeros((1, 32), f32)], axis=1)
            pieces = banded(jnp.broadcast_to(block, (8, 128)), lane8)
            for di in range(2):
                do = di - (a - 1) + 1
                for ro in range(4):
                    at = e * 16 + do * 4 + ro
                    w2b[at:at + 1, di * 128:(di + 1) * 128] = pieces[ro][0:1, :]

    fill(0, [(lt, 14, width - 8, 3, tl, 8)])
    fill(1, [(rt, 62, width - 8, 3, tr, 56)])
    lfull[8:width, :] = left_table((0, 1, 2), 8, width)
    right_table(56, width + 46)
    end_rows(0, 16, width)
    end_rows(1, 64, width)

    half = width // 2

    def hidden(d):
        if d == 0:
            return ends[0, half:width, :]
        if d == DISP - 1:
            return ends[1, half:width, :]
        s = DISP - 1 - d
        return jnp.maximum(lfull[half:width, :] + rfull[s + half:s + width, :], 0.0).astype(bf16)

    for k, (one, two, three) in cost_sums(w2b[...].astype(bf16), hidden):
        costs[k] = one + pltpu.roll(two, half - 1, 1) + pltpu.roll(three, half - 2, 1)


    @pl.when(has_left)
    def _():
        to_right.wait_recv()
        rt[0:56, :] = in_l[8:64, :].astype(f32)
        lt[0:8, :] = in_l[72:80, :].astype(f32)

    @pl.when(has_right)
    def _():
        to_left.wait_recv()
        rt[56 + width:64 + width, :] = in_r[0:8, :].astype(f32)
        lt[8 + width:16 + width, :] = in_r[16:24, :].astype(f32)

    fill(1, [(rt, 6, 56, 3, tr, 0), (rt, width + 54, 16, 3, tr, width + 48), (rt, width + 6, 64, 2, te, 0)])
    fill(0, [(lt, 6, 8, 3, tl, 0), (lt, width + 6, 8, 3, tl, width)])
    halo_out[...] = jnp.concatenate([jnp.zeros((8, 128), f32), rt[0:56, :]], axis=0).T.astype(bf16)

    lfull[0:8, :] = left_table((0, 1, 2), 0, 8)
    lfull[width:width + 8, :] = left_table((0, 1, 2), width, width + 8)
    lfull[width + 8:width + 16, :] = jnp.full((8, 128), NEG, f32)
    right_table(0, 56)
    right_table(width + 40, width + 56)
    edge = te[0, 2:58, :] + te[1, 1:57, :] + te[2, 0:56, :]
    rtail[0:56, :] = jnp.where(last, edge, rfull[width:width + 56, :])
    rtail[56:64, :] = jnp.zeros((8, 128), f32)
    end_rows(0, 0, 16)
    end_rows(1, 0, 64)
    for k, (a, b, s) in enumerate(end_taps):
        inner = tr[a, s + 1 + width:s + 9 + width, :] + tr[b, s + width:s + 8 + width, :]
        outer = te[a, s + 1:s + 9, :] + te[b, s:s + 8, :]
        tail = jnp.maximum(left_table((a, b), width, width + 8) + jnp.where(last, outer, inner), 0.0)
        ends[k, width:width + 16, :] = jnp.concatenate([tail, jnp.zeros((8, 128), f32)], axis=0).astype(bf16)

    @pl.when(has_right)
    def _():
        to_right.wait_send()

    @pl.when(has_left)
    def _():
        to_left.wait_send()


def cost_kernel(left_ref, right_ref, lfull, rfull, rtail, ends, w2b, halo_ref, costs,
                disp_hbm, conf_hbm, disp_ref, conf_ref, sem):
    rows, feat, width = left_ref.shape
    flat = rows * feat
    f32, bf16 = jnp.float32, jnp.bfloat16

    half = width // 2
    lo, hi = half + 8, width - 8

    def hidden(d):
        if d == 0 or d == DISP - 1:
            k = 0 if d == 0 else 1
            parts = [ends[k, 0:lo, :].astype(f32), ends[k, hi:width + 16, :].astype(f32)]
            return jnp.concatenate(parts, axis=0).astype(bf16)
        s = DISP - 1 - d
        parts = [
            lfull[0:lo, :] + rfull[s:s + lo, :],
            lfull[hi:width, :] + rfull[s + hi:s + width, :],
            lfull[width:width + 16, :] + rtail[s:s + 16, :],
        ]
        return jnp.maximum(jnp.concatenate(parts, axis=0), 0.0).astype(bf16)

    low = lax.broadcasted_iota(jnp.int32, (8, width), 0) < 4
    ready = lax.broadcasted_iota(jnp.int32, (8, half), 1) < half - 2
    total = jnp.zeros((8, width), jnp.float32)
    moment = jnp.zeros((8, width), jnp.float32)
    pairs = DISP // 2
    for k, sums in cost_sums(w2b[...].astype(bf16), hidden):
        near = sums[0][:, 0:half] + sums[1][:, 1:half + 1] + sums[2][:, 2:half + 2]
        edge = sums[0][:, 16:half + 16] + sums[1][:, 17:half + 17] + sums[2][:, 18:half + 18]
        cost = jnp.concatenate([near, jnp.where(ready, costs[k], edge)], axis=1)
        expo = jnp.exp(-cost)
        if k == 0:
            expo = jnp.where(low, 0.0, expo)
        elif k == pairs:
            expo = jnp.where(low, expo, 0.0)
        total = total + expo
        moment = moment + expo * float(2 * k - 1)
    soft = (moment[0:4, :] + moment[4:8, :] + total[4:8, :]) / (total[0:4, :] + total[4:8, :])
    disp_ref[...] = soft / DISP
    save_disp = pltpu.make_async_copy(disp_ref, disp_hbm, sem.at[0])
    save_disp.start()

    held = jnp.minimum(soft, float(DISP - 1))
    halo = halo_ref[...]
    left_nat = left_ref[...].reshape(flat, width)
    right_nat = right_ref[...].reshape(flat, width)
    gap = (lax.broadcasted_iota(jnp.int32, (192, half), 1) - lax.broadcasted_iota(jnp.int32, (192, half), 0) + 64).astype(jnp.float32)
    for r in range(rows):
        band = slice(feat * r, feat * (r + 1))
        for h in range(width // half):
            want = held[r:r + 1, h * half:(h + 1) * half]
            weight = jnp.maximum(0.0, 1.0 - jnp.abs(want - gap))
            head = weight.astype(jnp.bfloat16)
            rest = (weight - head.astype(jnp.float32)).astype(jnp.bfloat16)
            own = right_nat[band, h * half:(h + 1) * half]
            if h == 0:
                before = halo[band, :]
            else:
                before = right_nat[band, (h - 1) * half + 64:h * half]
            warped = jnp.zeros((feat, half), jnp.float32)
            for part in (head, rest):
                warped = warped + jnp.dot(before, part[0:64, :], preferred_element_type=jnp.float32)
                warped = warped + jnp.dot(own, part[64:192, :], preferred_element_type=jnp.float32)
            off = jnp.abs(left_nat[band, h * half:(h + 1) * half].astype(jnp.float32) - warped)
            error = jnp.sum(off, axis=0, keepdims=True) * (1.0 / feat)
            conf_ref[r:r + 1, h * half:(h + 1) * half] = jnp.exp(-error)
    save_conf = pltpu.make_async_copy(conf_ref, conf_hbm, sem.at[1])
    save_conf.start()
    save_disp.wait()
    save_conf.wait()


def on_device(left_feat, right_feat, w_first, w_second):
    rows, feat, width = left_feat.shape
    n = lax.axis_size("col")
    f32, bf16 = jnp.float32, jnp.bfloat16
    w_cost = w_second[:, :, :, 0, :]
    vmem = pl.BlockSpec(memory_space=pltpu.VMEM)
    hbm = pl.BlockSpec(memory_space=pltpu.HBM)
    shape = jax.ShapeDtypeStruct
    tables = pl.pallas_call(
        functools.partial(tables_kernel, n),
        out_shape=(
            shape(left_feat.shape, bf16),
            shape(right_feat.shape, bf16),
            shape((width + 16, 128), f32),
            shape((width + 56, 128), f32),
            shape((64, 128), f32),
            shape((2, width + 16, 128), bf16),
            shape((48, 256), f32),
            shape((128, 64), bf16),
            shape((DISP // 2 + 1, 8, width // 2), f32),
        ),
        in_specs=[hbm] * 4,
        out_specs=(vmem,) * 9,
        scratch_shapes=[
            pltpu.VMEM((width + 16, 128), f32),
            pltpu.VMEM((width + 72, 128), f32),
            pltpu.VMEM((2, 384, 384), bf16),
            pltpu.VMEM((3, width + 8, 128), f32),
            pltpu.VMEM((3, width + 64, 128), f32),
            pltpu.VMEM((3, 64, 128), f32),
            pltpu.VMEM(w_first.shape, bf16),
            pltpu.VMEM(w_cost.shape, bf16),
            pltpu.VMEM((80, 128), bf16),
            pltpu.VMEM((32, 128), bf16),
            pltpu.VMEM((80, 128), bf16),
            pltpu.VMEM((32, 128), bf16),
            pltpu.SemaphoreType.DMA((4,)),
            pltpu.SemaphoreType.DMA((2,)),
            pltpu.SemaphoreType.DMA((2,)),
        ],
        compiler_params=pltpu.CompilerParams(
            collective_id=0, has_side_effects=True, vmem_limit_bytes=16 << 20),
    )(*(pltpu.with_memory_space_constraint(x, pltpu.HBM) for x in (left_feat, right_feat, w_first, w_cost)))
    out = shape((rows, width), f32)
    return pl.pallas_call(
        cost_kernel,
        out_shape=(out, out),
        in_specs=[vmem] * 9,
        out_specs=(hbm, hbm),
        scratch_shapes=[
            pltpu.VMEM((rows, width), f32),
            pltpu.VMEM((rows, width), f32),
            pltpu.SemaphoreType.DMA((2,)),
        ],
        compiler_params=pltpu.CompilerParams(vmem_limit_bytes=16 << 20),
    )(*tables)


def solution(mesh):
    in_specs = (P("band", None, "col"), P("band", None, "col"), P(), P())
    out_specs = (P("band", "col"), P("band", "col"))
    return jax.shard_map(
        on_device, mesh=mesh, in_specs=in_specs, out_specs=out_specs, check_vma=False
    )
```

```python
import functools

import jax
import jax.numpy as jnp
from jax import lax
from jax.experimental import pallas as pl
from jax.experimental.pallas import tpu as pltpu
from jax.sharding import PartitionSpec as P

DISP = 48
NEG = -1e30
NT = (((1,), (1,)), ((), ()))
MESH = pl.DeviceIdType.MESH


def banded(block, lane):
    return [
        jnp.where(lane < 64, pltpu.roll(block, 96, 1), 0.0),
        block,
        pltpu.roll(block, 32, 1),
        jnp.where(lane >= 64, pltpu.roll(block, 64, 1), 0.0),
    ]


def cost_sums(weights, hidden):
    carry = None
    pairs = DISP // 2
    for k in range(pairs + 1):
        if k < pairs:
            both = jnp.concatenate([hidden(2 * k), hidden(2 * k + 1)], axis=1)
            q = lax.dot_general(weights, both, NT, preferred_element_type=jnp.float32)
            lows = [q[16 * e:16 * e + 8, :] for e in range(3)]
            highs = [q[16 * e + 8:16 * e + 16, :] for e in range(3)]
        if k == 0:
            sums = lows
        elif k == pairs:
            sums = carry
        else:
            sums = [x + y for x, y in zip(lows, carry)]
        carry = highs
        yield k, sums


def tables_kernel(n, left_hbm, right_hbm, w1_hbm, w2_hbm,
                  left_out, right_out, lfull, rfull, rtail, ends, w2b, halo_out, costs,
                  lt, rt, wb, tl, tr, te, w1_ref, w2_ref, out_r, out_l, in_l, in_r, load_sem, send_sem, recv_sem):
    rows, feat, width = left_out.shape
    flat = rows * feat
    f32, bf16 = jnp.float32, jnp.bfloat16
    col = lax.axis_index("col")
    has_left = col > 0
    has_right = col < n - 1
    left_id = {"col": jnp.maximum(col - 1, 0)}
    right_id = {"col": jnp.minimum(col + 1, n - 1)}
    first = col == 0
    last = col == n - 1

    barrier = pltpu.get_barrier_semaphore()

    @pl.when(has_left)
    def _():
        pl.semaphore_signal(barrier, inc=1, device_id=left_id, device_id_type=MESH)

    @pl.when(has_right)
    def _():
        pl.semaphore_signal(barrier, inc=1, device_id=right_id, device_id_type=MESH)

    loads = [
        pltpu.make_async_copy(src, dst, load_sem.at[i])
        for i, (src, dst) in enumerate(
            ((right_hbm, right_out), (left_hbm, left_out), (w1_hbm, w1_ref), (w2_hbm, w2_ref)))
    ]
    for c in loads:
        c.start()

    rt[64 + width:72 + width, :] = jnp.zeros((8, flat), f32)

    @pl.when(first)
    def _():
        rt[0:56, :] = jnp.zeros((56, flat), f32)
        lt[0:8, :] = jnp.zeros((8, flat), f32)

    @pl.when(last)
    def _():
        rt[56 + width:64 + width, :] = jnp.zeros((8, flat), f32)
        lt[8 + width:16 + width, :] = jnp.zeros((8, flat), f32)

    w2b[...] = jnp.zeros_like(w2b)

    def copy(index, src, dst, target):
        return pltpu.make_async_remote_copy(
            src_ref=src, dst_ref=dst, send_sem=send_sem.at[index], recv_sem=recv_sem.at[index],
            device_id=target, device_id_type=MESH)

    to_right = copy(0, out_r, in_l, right_id)
    to_left = copy(1, out_l, in_r, left_id)

    def turned(ref, lo, hi):
        return ref[:, :, lo:hi].reshape(flat, hi - lo).astype(f32).T

    loads[0].wait()
    r_tail = turned(right_out, width - 128, width)
    out_r[0:64, :] = r_tail[64:128, :].astype(bf16)
    loads[1].wait()
    l_tail = turned(left_out, width - 128, width)
    out_r[64:80, :] = l_tail[112:128, :].astype(bf16)

    pl.semaphore_wait(barrier, has_left.astype(jnp.int32) + has_right.astype(jnp.int32))

    @pl.when(has_right)
    def _():
        to_right.start()

    r_head = turned(right_out, 0, width - 128)
    l_head = turned(left_out, 0, width - 128)
    out_l[0:16, :] = r_head[0:16, :].astype(bf16)
    out_l[16:32, :] = l_head[0:16, :].astype(bf16)

    @pl.when(has_left)
    def _():
        to_left.start()

    rt[56:width - 72, :] = r_head
    rt[width - 72:width + 56, :] = r_tail
    lt[8:width - 120, :] = l_head
    lt[width - 120:width + 8, :] = l_tail

    loads[2].wait()
    lane = lax.broadcasted_iota(jnp.int32, (32, 128), 1)
    zero = jnp.zeros((32, 32), f32)
    for a in range(3):
        for e in range(3):
            taps = [w1_ref[a, b, e].astype(f32) for b in range(3)]
            for side in range(2):
                block = jnp.concatenate([t[:, 32 * side:32 * side + 32] for t in taps] + [zero], axis=1)
                for ro, piece in enumerate(banded(block, lane)):
                    at = a * 128 + ro * 32
                    wb[side, at:at + 32, e * 128:(e + 1) * 128] = piece.astype(bf16)

    def shifted(ref, start, count, used=3):
        parts = [ref[start + e:start + e + count, :].astype(bf16) for e in range(used)]
        return jnp.concatenate(parts + [jnp.zeros((count, 128), bf16)] * (3 - used), axis=1)

    def fill(side, pieces):
        lhs = [shifted(ref, start, count, used) for ref, start, count, used, _, _ in pieces]
        lhs = lhs[0] if len(lhs) == 1 else jnp.concatenate(lhs, axis=0)
        res = lax.dot_general(lhs, wb[side], NT, preferred_element_type=f32)
        at = 0
        for _, _, count, _, out, to in pieces:
            for a in range(3):
                out[a, to:to + count, :] = res[at:at + count, a * 128:(a + 1) * 128]
            at += count

    def left_table(taps, lo, hi):
        value = sum(tl[a, lo:hi, :] for a in taps)
        line = lo + lax.broadcasted_iota(jnp.int32, (hi - lo, 128), 0)
        dead = (first & (line == 0)) | (last & (line >= width + 1))
        return jnp.where(dead, NEG, value)

    def right_table(lo, hi):
        rfull[lo:hi, :] = tr[0, lo + 2:hi + 2, :] + tr[1, lo + 1:hi + 1, :] + tr[2, lo:hi, :]

    end_taps = ((1, 2, DISP - 1), (0, 1, 1))

    def end_rows(k, lo, hi):
        a, b, s = end_taps[k]
        body = tr[a, s + 1 + lo:s + 1 + hi, :] + tr[b, s + lo:s + hi, :]
        ends[k, lo:hi, :] = jnp.maximum(left_table((a, b), lo, hi) + body, 0.0).astype(bf16)

    loads[3].wait()
    lane8 = lax.broadcasted_iota(jnp.int32, (8, 128), 1)
    for a in range(3):
        for e in range(3):
            taps = [w2_ref[a, b, e:e + 1, :].astype(f32) for b in range(3)]
            block = jnp.concatenate(taps + [jnp.zeros((1, 32), f32)], axis=1)
            pieces = banded(jnp.broadcast_to(block, (8, 128)), lane8)
            for di in range(2):
                do = di - (a - 1) + 1
                for ro in range(4):
                    at = e * 16 + do * 4 + ro
                    w2b[at:at + 1, di * 128:(di + 1) * 128] = pieces[ro][0:1, :]

    fill(0, [(lt, 14, width - 8, 3, tl, 8)])
    fill(1, [(rt, 62, width - 8, 3, tr, 56)])
    lfull[8:width, :] = left_table((0, 1, 2), 8, width)
    right_table(56, width + 46)
    end_rows(0, 16, width)
    end_rows(1, 64, width)

    half = width // 2

    def hidden(d):
        if d == 0:
            return ends[0, half:width, :]
        if d == DISP - 1:
            return ends[1, half:width, :]
        s = DISP - 1 - d
        return jnp.maximum(lfull[half:width, :] + rfull[s + half:s + width, :], 0.0).astype(bf16)

    for k, (one, two, three) in cost_sums(w2b[...].astype(bf16), hidden):
        costs[k] = one + pltpu.roll(two, half - 1, 1) + pltpu.roll(three, half - 2, 1)


    @pl.when(has_left)
    def _():
        to_right.wait_recv()
        rt[0:56, :] = in_l[8:64, :].astype(f32)
        lt[0:8, :] = in_l[72:80, :].astype(f32)

    @pl.when(has_right)
    def _():
        to_left.wait_recv()
        rt[56 + width:64 + width, :] = in_r[0:8, :].astype(f32)
        lt[8 + width:16 + width, :] = in_r[16:24, :].astype(f32)

    fill(1, [(rt, 6, 56, 3, tr, 0), (rt, width + 54, 16, 3, tr, width + 48), (rt, width + 6, 64, 2, te, 0)])
    fill(0, [(lt, 6, 8, 3, tl, 0), (lt, width + 6, 8, 3, tl, width)])
    halo_out[...] = jnp.concatenate([jnp.zeros((72, 128), f32), rt[0:56, :]], axis=0).T.astype(bf16)

    lfull[0:8, :] = left_table((0, 1, 2), 0, 8)
    lfull[width:width + 8, :] = left_table((0, 1, 2), width, width + 8)
    lfull[width + 8:width + 16, :] = jnp.full((8, 128), NEG, f32)
    right_table(0, 56)
    right_table(width + 40, width + 56)
    edge = te[0, 2:58, :] + te[1, 1:57, :] + te[2, 0:56, :]
    rtail[0:56, :] = jnp.where(last, edge, rfull[width:width + 56, :])
    rtail[56:64, :] = jnp.zeros((8, 128), f32)
    end_rows(0, 0, 16)
    end_rows(1, 0, 64)
    for k, (a, b, s) in enumerate(end_taps):
        inner = tr[a, s + 1 + width:s + 9 + width, :] + tr[b, s + width:s + 8 + width, :]
        outer = te[a, s + 1:s + 9, :] + te[b, s:s + 8, :]
        tail = jnp.maximum(left_table((a, b), width, width + 8) + jnp.where(last, outer, inner), 0.0)
        ends[k, width:width + 16, :] = jnp.concatenate([tail, jnp.zeros((8, 128), f32)], axis=0).astype(bf16)

    @pl.when(has_right)
    def _():
        to_right.wait_send()

    @pl.when(has_left)
    def _():
        to_left.wait_send()


def cost_kernel(left_ref, right_ref, lfull, rfull, rtail, ends, w2b, halo_ref, costs,
                disp_hbm, conf_hbm, disp_ref, conf_ref, sem):
    rows, feat, width = left_ref.shape
    flat = rows * feat
    f32, bf16 = jnp.float32, jnp.bfloat16

    half = width // 2
    lo, hi = half + 8, width - 8

    def hidden(d):
        if d == 0 or d == DISP - 1:
            k = 0 if d == 0 else 1
            parts = [ends[k, 0:lo, :].astype(f32), ends[k, hi:width + 16, :].astype(f32)]
            return jnp.concatenate(parts, axis=0).astype(bf16)
        s = DISP - 1 - d
        parts = [
            lfull[0:lo, :] + rfull[s:s + lo, :],
            lfull[hi:width, :] + rfull[s + hi:s + width, :],
            lfull[width:width + 16, :] + rtail[s:s + 16, :],
        ]
        return jnp.maximum(jnp.concatenate(parts, axis=0), 0.0).astype(bf16)

    low = lax.broadcasted_iota(jnp.int32, (8, width), 0) < 4
    ready = lax.broadcasted_iota(jnp.int32, (8, half), 1) < half - 2
    total = jnp.zeros((8, width), jnp.float32)
    moment = jnp.zeros((8, width), jnp.float32)
    pairs = DISP // 2
    for k, sums in cost_sums(w2b[...].astype(bf16), hidden):
        near = sums[0][:, 0:half] + sums[1][:, 1:half + 1] + sums[2][:, 2:half + 2]
        edge = sums[0][:, 16:half + 16] + sums[1][:, 17:half + 17] + sums[2][:, 18:half + 18]
        cost = jnp.concatenate([near, jnp.where(ready, costs[k], edge)], axis=1)
        expo = jnp.exp(-cost)
        if k == 0:
            expo = jnp.where(low, 0.0, expo)
        elif k == pairs:
            expo = jnp.where(low, expo, 0.0)
        total = total + expo
        moment = moment + expo * float(2 * k - 1)
    soft = (moment[0:4, :] + moment[4:8, :] + total[4:8, :]) / (total[0:4, :] + total[4:8, :])
    disp_ref[...] = soft / DISP
    save_disp = pltpu.make_async_copy(disp_ref, disp_hbm, sem.at[0])
    save_disp.start()

    held = jnp.minimum(soft, float(DISP - 1))
    halo = halo_ref[...]
    left_nat = left_ref[...].reshape(flat, width)
    right_nat = right_ref[...].reshape(flat, width)
    gap = (lax.broadcasted_iota(jnp.int32, (192, half), 1) - lax.broadcasted_iota(jnp.int32, (192, half), 0) + 64).astype(jnp.float32)
    blank = jnp.zeros((64, half), jnp.bfloat16)
    for r in range(rows):
        band = slice(feat * r, feat * (r + 1))
        for h in range(width // half):
            want = held[r:r + 1, h * half:(h + 1) * half]
            weight = jnp.maximum(0.0, 1.0 - jnp.abs(want - gap))
            head = weight.astype(jnp.bfloat16)
            rest = (weight - head.astype(jnp.float32)).astype(jnp.bfloat16)
            if h == 0:
                cols = jnp.concatenate([halo[band, :], right_nat[band, 0:half]], axis=1)
            else:
                cols = right_nat[band, (h - 1) * half:(h + 1) * half]
            warped = jnp.zeros((feat, half), jnp.float32)
            for part in (head, rest):
                part = jnp.concatenate([blank, part], axis=0)
                warped = warped + jnp.dot(cols, part, preferred_element_type=jnp.float32)
            off = jnp.abs(left_nat[band, h * half:(h + 1) * half].astype(jnp.float32) - warped)
            error = jnp.sum(off, axis=0, keepdims=True) * (1.0 / feat)
            conf_ref[r:r + 1, h * half:(h + 1) * half] = jnp.exp(-error)
    save_conf = pltpu.make_async_copy(conf_ref, conf_hbm, sem.at[1])
    save_conf.start()
    save_disp.wait()
    save_conf.wait()


def on_device(left_feat, right_feat, w_first, w_second):
    rows, feat, width = left_feat.shape
    n = lax.axis_size("col")
    f32, bf16 = jnp.float32, jnp.bfloat16
    w_cost = w_second[:, :, :, 0, :]
    vmem = pl.BlockSpec(memory_space=pltpu.VMEM)
    hbm = pl.BlockSpec(memory_space=pltpu.HBM)
    shape = jax.ShapeDtypeStruct
    tables = pl.pallas_call(
        functools.partial(tables_kernel, n),
        out_shape=(
            shape(left_feat.shape, bf16),
            shape(right_feat.shape, bf16),
            shape((width + 16, 128), f32),
            shape((width + 56, 128), f32),
            shape((64, 128), f32),
            shape((2, width + 16, 128), bf16),
            shape((48, 256), f32),
            shape((128, 128), bf16),
            shape((DISP // 2 + 1, 8, width // 2), f32),
        ),
        in_specs=[hbm] * 4,
        out_specs=(vmem,) * 9,
        scratch_shapes=[
            pltpu.VMEM((width + 16, 128), f32),
            pltpu.VMEM((width + 72, 128), f32),
            pltpu.VMEM((2, 384, 384), bf16),
            pltpu.VMEM((3, width + 8, 128), f32),
            pltpu.VMEM((3, width + 64, 128), f32),
            pltpu.VMEM((3, 64, 128), f32),
            pltpu.VMEM(w_first.shape, bf16),
            pltpu.VMEM(w_cost.shape, bf16),
            pltpu.VMEM((80, 128), bf16),
            pltpu.VMEM((32, 128), bf16),
            pltpu.VMEM((80, 128), bf16),
            pltpu.VMEM((32, 128), bf16),
            pltpu.SemaphoreType.DMA((4,)),
            pltpu.SemaphoreType.DMA((2,)),
            pltpu.SemaphoreType.DMA((2,)),
        ],
        compiler_params=pltpu.CompilerParams(
            collective_id=0, has_side_effects=True, vmem_limit_bytes=16 << 20),
    )(*(pltpu.with_memory_space_constraint(x, pltpu.HBM) for x in (left_feat, right_feat, w_first, w_cost)))
    out = shape((rows, width), f32)
    return pl.pallas_call(
        cost_kernel,
        out_shape=(out, out),
        in_specs=[vmem] * 9,
        out_specs=(hbm, hbm),
        scratch_shapes=[
            pltpu.VMEM((rows, width), f32),
            pltpu.VMEM((rows, width), f32),
            pltpu.SemaphoreType.DMA((2,)),
        ],
        compiler_params=pltpu.CompilerParams(vmem_limit_bytes=16 << 20),
    )(*tables)


def solution(mesh):
    in_specs = (P("band", None, "col"), P("band", None, "col"), P(), P())
    out_specs = (P("band", "col"), P("band", "col"))
    return jax.shard_map(
        on_device, mesh=mesh, in_specs=in_specs, out_specs=out_specs, check_vma=False
    )
```
